32 devices in a mesh: groups: 2 (over x), dom: 16 (over z, y, core).
Axes of the slice: x: 2, y: 2, z: 4, core: 2. Of those that a mesh axis runs over, the one named last changes fastest.
Arguments:
- micrographs: bfloat16 [64, 1024, 1024], P(('groups', 'dom')), parts along dimension 0, may hold values from -6 to 6
- mic_defocus: int32 [64], P(('groups', 'dom')), parts along dimension 0, may hold values from 0 to 15
- defocus: float32 [32], P('groups'), parts along dimension 0, may hold values from 0.5 to 3
- pick_list: int32 [4, 6144], P(None, ('groups', 'dom')), parts along dimension 1, may hold values from -1 to 1535, as said below
- template_bank: bfloat16 [448, 2048], P(('groups', 'dom')), parts along dimension 0, may hold values from -0.125 to 0.125
- rot_index: int32 [100, 36], P('groups'), parts along dimension 0, may hold values from 0 to 223, as said below
Outputs:
- correlation: bfloat16 [3072, 16, 1800], P(('groups', 'dom')), parts along dimension 0
The draws below stay inside these ranges and needn't reach their ends.
There are 2 independent parts, one for each index of `groups`. The reference program is written for one: setup_inputs(seed, part) draws one part's arguments, and reference() takes and returns one part's arrays. A program takes and returns all parts, laid end to end along the dimension named above; each array names one. Nothing has to cross between parts.
Inputs may be any that keep to these rules, and one draw needn't show every extreme that they name: `pick_list`: row 0 is a micrograph of the device that holds the column (its local index), rows 1 and 2 the top-left pixel of a 256 x 256 box inside it, row 3 the particle the box becomes or -1 for an unused column. Every particle is named by exactly one column. The used columns of one device that name particles of one device number 0 or exactly 12; a device has at most 192 used columns, reached on a quarter of the devices. `rot_index`: every bank entry is named at least once.
All inputs are finite; a program needn't handle non-finite values.
Results may differ from the reference program's by a relative error of at most 0.0071.
Values may be sent and summed in bfloat16 or wider, within the bound.
A program may use at most 128 MiB of HBM per device.

```python
import math
import jax
import jax.numpy as jnp
from jax import lax

BOX = 256
K = 32
CLASSES = 50
ROTS = 36
SH = 4
DEFOCI = 16
MIC = 1024
MICS_DEV = 2
P_DEV = 96
TEMPLATES = 1800
SHIFTS = 16
CAP = 12
PICK_CAP = 192
PICKS = 3072
MICS = 32
BANK = 224
N_DOM = 16


def draw_pick_list(key, part):
    group_count = P_DEV // CAP
    half_groups = group_count // 2
    quarter = N_DOM // 4
    remainder = N_DOM - quarter
    total = P_DEV * N_DOM
    key_src, key_slot, key_rows, key_mic, key_top, key_left = jax.random.split(key, 6)
    source_order = jax.random.permutation(key_src, N_DOM)
    heavy_set = source_order[:quarter]
    light_set = source_order[quarter:]
    target_dev = jnp.arange(N_DOM, dtype=jnp.int32)[:, None]
    group_ids = jnp.arange(group_count, dtype=jnp.int32)[None, :]
    heavy_pick = heavy_set[jnp.mod(target_dev + group_ids, quarter)]
    light_pick = light_set[jnp.mod(target_dev + group_ids - half_groups, remainder)]
    group_source = jnp.where(group_ids < half_groups, heavy_pick, light_pick)
    slot_keys = jax.random.split(key_slot, N_DOM)
    slot_perm = jax.vmap(lambda one_key: jax.random.permutation(one_key, P_DEV))(slot_keys)
    slot_source = jnp.take_along_axis(group_source, slot_perm // CAP, axis=1).reshape(-1).astype(jnp.int32)
    order_idx = jnp.argsort(slot_source, stable=True).astype(jnp.int32)
    sorted_source = slot_source[order_idx]
    per_source = jnp.sum((slot_source[None, :] == jnp.arange(N_DOM, dtype=jnp.int32)[:, None]).astype(jnp.int32), axis=1)
    starts = jnp.cumsum(per_source) - per_source
    within = jnp.arange(total, dtype=jnp.int32) - starts[sorted_source]
    row_keys = jax.random.split(key_rows, N_DOM)
    row_perm = jax.vmap(lambda one_key: jax.random.permutation(one_key, PICK_CAP))(row_keys)
    column = sorted_source * PICK_CAP + row_perm[sorted_source, within]
    target_row = jnp.full((PICKS,), -1, jnp.int32).at[column].set(order_idx)
    mic_row = jax.random.randint(key_mic, (PICKS,), 0, MICS_DEV)
    top_row = jax.random.randint(key_top, (PICKS,), 0, MIC - BOX + 1)
    left_row = jax.random.randint(key_left, (PICKS,), 0, MIC - BOX + 1)
    return jnp.stack([mic_row, top_row, left_row, target_row]).astype(jnp.int32)


def draw_rot_index(key, part):
    shuffled = jax.random.permutation(key, TEMPLATES)
    return jnp.mod(shuffled, BANK).reshape(CLASSES, ROTS).astype(jnp.int32)


def place_ends(values, rng, least, high):
    longest = values.shape.index(max(values.shape))
    spots = []
    for shift in (0, 1):
        where = [jax.random.randint(jax.random.fold_in(rng, axis), (), 0, length) for axis, length in enumerate(values.shape)]
        where[longest] = (where[longest] + shift) % values.shape[longest]
        spots.append(tuple(where))
    return values.at[spots[0]].set(least).at[spots[1]].set(high)


def shard_levels(own_key, dims, cuts, smallest, top_value):
    factor_of, own = 1.0, jax.random.fold_in(own_key, 6)
    for position, parts in cuts:
        draws = jnp.exp(jax.random.uniform(jax.random.fold_in(own, position), (parts,), jnp.float32, smallest / len(cuts), top_value / len(cuts)))
        factor_of = factor_of * jnp.repeat(draws, dims[position] // parts).reshape([-1 if axis == position else 1 for axis in range(len(dims))])
    return factor_of


def gaussian(own_key, extent, width, limit, pieces=(), kind=jnp.bfloat16):
    level = shard_levels(own_key, extent, pieces, -0.22, 0.18) if pieces else 1.0
    entries = jax.random.normal(own_key, extent, jnp.float32) * width * level
    return jnp.minimum(jnp.maximum(entries, -limit), limit).astype(kind)


def setup_inputs(seed: int = 0, part: int = 0) -> dict:
    arg_keys = jax.random.split(jax.random.key(seed), 7)
    part_splits = jax.random.split(jax.random.fold_in(arg_keys[6], part), 7)
    micrographs = gaussian(part_splits[0], (MICS, MIC, MIC), 1.0, 6.0, ((0, 16),))
    mic_defocus = place_ends(jax.random.randint(part_splits[1], (MICS,), 0, DEFOCI), jax.random.fold_in(part_splits[1], 1), 0, DEFOCI - 1).astype(jnp.int32)
    defocus = jnp.clip(jnp.exp(jax.random.uniform(part_splits[2], (DEFOCI,), jnp.float32, math.log(0.5), math.log(3.0))), 0.5, 3.0)
    pick_list = draw_pick_list(jax.random.fold_in(jax.random.fold_in(arg_keys[6], part), 71), part)
    template_bank = gaussian(part_splits[4], (BANK, 2 * K * K), (2 * K * K) ** -0.5, 0.125, ((0, 16),))
    rot_index = draw_rot_index(jax.random.fold_in(jax.random.fold_in(arg_keys[6], part), 71), part)
    return {"micrographs": micrographs, "mic_defocus": mic_defocus, "defocus": defocus, "pick_list": pick_list, "template_bank": template_bank, "rot_index": rot_index}


TWO_PI = 2.0 * math.pi
CHI_SCALE = 0.05
CHI_SHIFT = 0.1

def forward_table(box_side, freq_side):
    offsets = jnp.arange(freq_side, dtype=jnp.int32) - freq_side // 2
    pixels = jnp.arange(box_side, dtype=jnp.int32)
    phase_turns = jnp.mod(offsets[:, None] * pixels[None, :], box_side).astype(jnp.float32) / box_side
    norm_scale = 1.0 / math.sqrt(box_side)
    stacked = jnp.concatenate([jnp.cos(TWO_PI * phase_turns) * norm_scale, -jnp.sin(TWO_PI * phase_turns) * norm_scale], axis=0)
    return stacked.astype(jnp.bfloat16)

def ctf_table(defocus, freq_side):
    offsets = (jnp.arange(freq_side, dtype=jnp.int32) - freq_side // 2).astype(jnp.float32)
    radius = (offsets[:, None] * offsets[:, None] + offsets[None, :] * offsets[None, :]).reshape(-1)
    return -jnp.sin(CHI_SCALE * defocus[:, None] * radius[None, :] + CHI_SHIFT)

def shift_tables(box_side, freq_side, shift_side):
    offsets = jnp.arange(freq_side, dtype=jnp.int32) - freq_side // 2
    shift_moves = jnp.arange(shift_side, dtype=jnp.int32) - shift_side // 2
    row_freq = jnp.repeat(offsets, freq_side)
    col_freq = jnp.tile(offsets, freq_side)
    row_move = jnp.repeat(shift_moves, shift_side)
    col_move = jnp.tile(shift_moves, shift_side)
    phase_turns = jnp.mod(row_move[:, None] * row_freq[None, :] + col_move[:, None] * col_freq[None, :], box_side).astype(jnp.float32) / box_side
    return (jnp.cos(TWO_PI * phase_turns), jnp.sin(TWO_PI * phase_turns))

def spectra(box_stack, dft_table, ctf_rows, freq_side):
    first_pass = jnp.einsum('ky,byx->bkx', dft_table.astype(jnp.float32), box_stack.astype(jnp.float32), precision=lax.Precision.HIGHEST).astype(jnp.bfloat16)
    second = jnp.einsum('bkx,jx->bkj', first_pass.astype(jnp.float32), dft_table.astype(jnp.float32), precision=lax.Precision.HIGHEST)
    real_part = second[:, :freq_side, :freq_side] - second[:, freq_side:, freq_side:]
    imag_part = second[:, :freq_side, freq_side:] + second[:, freq_side:, :freq_side]
    box_count = box_stack.shape[0]
    joined = jnp.concatenate([real_part.reshape(box_count, -1) * ctf_rows, imag_part.reshape(box_count, -1) * ctf_rows], axis=1)
    return joined.astype(jnp.bfloat16)

def shift_rows(window, cosine, sine_part, freq_side):
    box_count = window.shape[0]
    freq_area = freq_side * freq_side
    real_w = window[:, :freq_area].astype(jnp.float32)[:, None, :]
    imag_w = window[:, freq_area:].astype(jnp.float32)[:, None, :]
    real_s = real_w * cosine[None] - imag_w * sine_part[None]
    imag_s = real_w * sine_part[None] + imag_w * cosine[None]
    joined = jnp.concatenate([real_s, imag_s], axis=2).astype(jnp.bfloat16)
    return joined.reshape(box_count * cosine.shape[0], 2 * freq_area)

def reference(micrographs, mic_defocus, defocus, pick_list, template_bank, rot_index):
    total = P_DEV * N_DOM
    target_index = pick_list[3]
    column_count = target_index.shape[0]
    placed = jnp.where(target_index >= 0, target_index, total)
    row_of = jnp.zeros((total,), jnp.int32).at[placed].set(jnp.arange(column_count, dtype=jnp.int32), mode='drop')
    owner = (row_of // PICK_CAP).astype(jnp.int32)
    mic_global = (owner * MICS_DEV + pick_list[0][row_of]).astype(jnp.int32)
    top_rows = pick_list[1][row_of].astype(jnp.int32)
    left_cols = pick_list[2][row_of].astype(jnp.int32)
    defocus_ids = mic_defocus[mic_global]
    dft_table = forward_table(BOX, K)
    ctf_all = ctf_table(defocus, K)
    cosine, sine_part = shift_tables(BOX, K, SH)
    templates = template_bank[rot_index.reshape(-1)]

    def crop_one(mic_id, top_row, left_col):
        return lax.dynamic_slice(micrographs, (mic_id, top_row, left_col), (1, BOX, BOX))[0]

    def one_block(block_args):
        mic_b, top_b, left_b, id_b = block_args
        box_stack = jax.vmap(crop_one)(mic_b, top_b, left_b)
        window = spectra(box_stack, dft_table, ctf_all[id_b], K)
        shifted = shift_rows(window, cosine, sine_part, K)
        scores = jnp.dot(shifted, templates.T, preferred_element_type=jnp.float32).astype(jnp.bfloat16)
        return scores.reshape(P_DEV, SHIFTS, TEMPLATES)
    result = lax.map(one_block, (mic_global.reshape(N_DOM, P_DEV), top_rows.reshape(N_DOM, P_DEV), left_cols.reshape(N_DOM, P_DEV), defocus_ids.reshape(N_DOM, P_DEV)))
    return result.reshape(total, SHIFTS, TEMPLATES)
```

```python
import functools
import math

import jax
import jax.numpy as jnp
import ml_dtypes
import numpy as np
from jax import lax
from jax.experimental import pallas as pl
from jax.experimental.pallas import tpu as pltpu
from jax.sharding import PartitionSpec as P

BOX = 256
K = 32
SH = 4
P_DEV = 96
SHIFTS = SH * SH
LANES = 128
ROWS = 16
GROUP = 4
CHUNK = 16

TWO_PI = 2.0 * math.pi
CHI_SCALE = 0.05
CHI_SHIFT = 0.1

SUB = np.arange(8)[:, None]
LANE = np.arange(LANES)[None, :]
TILE_U = (8 * (LANE // K) + SUB - K // 2).astype(np.float64)
TILE_V = (LANE % K + 0 * SUB - K // 2).astype(np.float64)


def dft_tables():
    freq = np.arange(K) - K // 2
    phase = TWO_PI * np.mod(freq[:, None] * np.arange(BOX)[None, :], BOX) / BOX
    cosine = np.cos(phase) / math.sqrt(BOX)
    sine = -np.sin(phase) / math.sqrt(BOX)
    left = np.concatenate([cosine, sine], axis=0)
    right = np.zeros((GROUP, BOX, 2 * GROUP * K))
    for j in range(GROUP):
        right[j, :, j * K : (j + 1) * K] = cosine.T
        right[j, :, GROUP * K + j * K : GROUP * K + (j + 1) * K] = sine.T
    right = right.reshape(GROUP * BOX, 2 * GROUP * K)
    return left.astype(np.float32).astype(ml_dtypes.bfloat16), right.astype(np.float32).astype(ml_dtypes.bfloat16)


def phase_tables():
    rows = TWO_PI * np.arange(ROWS)[:, None, None] * TILE_U[None] / BOX
    cols = TWO_PI * np.arange(LANES)[:, None] * TILE_V[:1] / BOX
    return [f(x).astype(np.float32) for x in (rows, cols) for f in (np.cos, np.sin)]


def shift_phases():
    moves = np.arange(SH) - SH // 2
    row_move = np.repeat(moves, SH)[None, :, None]
    col_move = np.tile(moves, SH)[None, :, None]
    phase = TWO_PI * (TILE_U[:, None, :] * row_move + TILE_V[:, None, :] * col_move) / BOX
    return np.cos(phase).astype(np.float32), np.sin(phase).astype(np.float32)


def bits(n):
    return (n - 1).bit_length()


def window_tiles(q, base, slot_cap, label_bits, row_bits, col_bits, info, mic_def, mic, lane_id, row_id, lhs):
    scalars = []
    last_tile = mic.shape[1] // ROWS - 1
    last_block = mic.shape[2] // LANES - 1
    for j in range(GROUP):
        packed = lax.shift_right_logical(info[base + j], label_bits)
        left = packed & (2**col_bits - 1)
        top = lax.shift_right_logical(packed, col_bits) & (2**row_bits - 1)
        m = lax.shift_right_logical(packed, col_bits + row_bits)
        block, rl = lax.shift_right_logical(left, 7), left & (LANES - 1)
        tile, rt = lax.shift_right_logical(top, 4), top & (ROWS - 1)
        end_tile = jnp.minimum(tile + BOX // ROWS, last_tile)
        row_f = rt.astype(jnp.float32).astype(jnp.bfloat16)
        col_f = rl.astype(jnp.float32).astype(jnp.bfloat16)

        def column(b):
            lanes = pl.ds(pl.multiple_of(b * LANES, LANES), LANES)
            main = mic[m, pl.ds(pl.multiple_of(tile * ROWS, ROWS), BOX), lanes]
            tail = mic[m, pl.ds(pl.multiple_of(end_tile * ROWS, ROWS), ROWS), lanes]
            head = jnp.where(row_id[...] >= row_f, main[:ROWS], tail)
            return jnp.concatenate([head, main[ROWS:]], axis=0)

        first = column(block)
        third = column(jnp.minimum(block + 2, last_block))
        mask = jnp.broadcast_to(lane_id[...], (BOX, LANES)) >= col_f
        lhs[pl.ds(q * BOX, BOX), pl.ds(2 * j * LANES, LANES)] = jnp.where(mask, first, third)
        lhs[pl.ds(q * BOX, BOX), pl.ds((2 * j + 1) * LANES, LANES)] = column(block + 1)
        scalars.append((m, rt, rl))
    return scalars


def group_windows(grid_part, scalars, left_t, prow_c, prow_s, pcol_c, pcol_s, ctf, mic_def):
    second = jnp.dot(left_t[...], grid_part.astype(jnp.bfloat16), preferred_element_type=jnp.float32)
    real = second[:K, :LANES] - second[K:, LANES:]
    imag = second[:K, LANES:] + second[K:, :LANES]
    block_id = lax.broadcasted_iota(jnp.int32, (8, LANES), 1) // K
    tiles = []
    for j in range(GROUP):
        parts = []
        for x in (real, imag):
            total = None
            for k in range(K // 8):
                piece = x[8 * k : 8 * k + 8]
                shift = (K * (k - j)) % LANES
                piece = pltpu.roll(piece, shift, 1) if shift else piece
                total = piece if total is None else jnp.where(block_id == k, piece, total)
            parts.append(total)
        m, rt, rl = scalars[j]
        cu, su = prow_c[rt], prow_s[rt]
        cv = jnp.broadcast_to(pcol_c[pl.ds(rl, 1), :], (8, LANES))
        sv = jnp.broadcast_to(pcol_s[pl.ds(rl, 1), :], (8, LANES))
        weight = ctf[mic_def[m]]
        a = (cu * cv - su * sv) * weight
        b = (su * cv + cu * sv) * weight
        tiles.append(
            jnp.concatenate(
                [parts[0] * a - parts[1] * b, parts[0] * b + parts[1] * a], axis=0
            ).astype(jnp.bfloat16)
        )
    return tiles


def crop_kernel(peers, slot_cap, shifts, info, mic_def, labels, mic, left_t, right_t, prow_c, prow_s,
                pcol_c, pcol_s, ctf, lane_id, row_id, out, lhs):
    groups = slot_cap // GROUP

    def per_peer(peer, carry):
        scalars = [
            window_tiles(q, peer * slot_cap + q * GROUP, slot_cap, *shifts, info, mic_def, mic,
                         lane_id, row_id, lhs)
            for q in range(groups)
        ]
        first = jnp.dot(lhs[...], right_t[...], preferred_element_type=jnp.float32)
        for q in range(groups):
            tiles = group_windows(first[q * BOX : (q + 1) * BOX], scalars[q], left_t, prow_c, prow_s,
                                  pcol_c, pcol_s, ctf, mic_def)
            for j in range(GROUP):
                out[peer, q * GROUP + j] = tiles[j]
        out[peer, slot_cap] = labels[peer]
        return carry

    lax.fori_loop(0, peers, per_peer, 0)


def score_kernel(where, arrived, bank, pick, cos_t, sin_t, out, lhs):
    base = pl.program_id(0) * CHUNK

    def expand(n, carry):
        x = arrived[where[base + n]].astype(jnp.float32)
        rows = pl.ds(pl.multiple_of(n * SHIFTS, SHIFTS), SHIFTS)
        for k in range(8):
            re = jnp.broadcast_to(x[k : k + 1], (SHIFTS, LANES))
            im = jnp.broadcast_to(x[8 + k : 9 + k], (SHIFTS, LANES))
            c, s = cos_t[k], sin_t[k]
            lhs[rows, k * LANES : (k + 1) * LANES] = (re * c - im * s).astype(jnp.bfloat16)
            lhs[rows, (8 + k) * LANES : (9 + k) * LANES] = (re * s + im * c).astype(jnp.bfloat16)
        return carry

    lax.fori_loop(0, CHUNK, expand, 0, unroll=2)
    scores = lax.dot_general(lhs[...], bank[...], (((1,), (1,)), ((), ())),
                             preferred_element_type=jnp.float32).astype(jnp.bfloat16)
    out[...] = jnp.dot(scores, pick[...], preferred_element_type=jnp.float32).astype(jnp.bfloat16)


VMEM = pl.BlockSpec(memory_space=pltpu.VMEM)
SMEM = pl.BlockSpec(memory_space=pltpu.SMEM)


def body(micrographs, mic_defocus, defocus, pick_list, template_bank, rot_index):
    peers = lax.axis_size("dom")
    slot_cap = (P_DEV + peers - 1) // peers * 2
    slot_cap = -(-slot_cap // GROUP) * GROUP
    mics, height, width = micrographs.shape
    label_bits, row_bits, col_bits = bits(P_DEV + 1), bits(height), bits(width)
    columns = pick_list.shape[1]

    target = pick_list[3]
    live = target >= 0
    target_dev = jnp.where(live, target // P_DEV, -1)
    label = jnp.where(live, jnp.mod(target, P_DEV) + 1, 0)
    ids = jnp.arange(columns, dtype=jnp.int32)
    earlier = (ids[None, :] < ids[:, None]) & (target_dev[None, :] == target_dev[:, None])
    rank = jnp.sum(earlier.astype(jnp.int32), axis=1)
    position = jnp.where(live, target_dev * slot_cap + rank, -1)
    mic_id = jnp.clip(pick_list[0], 0, mics - 1)
    top = jnp.clip(pick_list[1], 0, height - BOX)
    left = jnp.clip(pick_list[2], 0, width - BOX)
    packed = (((mic_id << row_bits) + top << col_bits) + left << label_bits) + label
    slots = jnp.arange(peers * slot_cap, dtype=jnp.int32)
    info = jnp.sum(jnp.where(position[None, :] == slots[:, None], packed[None, :], 0), axis=1)
    labels = (info & (2**label_bits - 1)).astype(jnp.bfloat16).reshape(peers, 1, slot_cap)
    labels = jnp.broadcast_to(jnp.pad(labels, ((0, 0), (0, 0), (0, LANES - slot_cap))), (peers, ROWS, LANES))

    left_t, right_t = dft_tables()
    radius = jnp.asarray((TILE_U**2 + TILE_V**2).astype(np.float32))
    ctf = -jnp.sin(CHI_SCALE * defocus[:, None, None] * radius[None] + CHI_SHIFT)
    lane_id = np.broadcast_to(np.arange(LANES, dtype=np.float32), (ROWS, LANES)).astype(ml_dtypes.bfloat16)
    row_id = np.broadcast_to(np.arange(ROWS, dtype=np.float32)[:, None], (ROWS, LANES)).astype(ml_dtypes.bfloat16)

    groups = slot_cap // GROUP
    outgoing = pl.pallas_call(
        functools.partial(crop_kernel, peers, slot_cap, (label_bits, row_bits, col_bits)),
        out_shape=jax.ShapeDtypeStruct((peers, slot_cap + 1, ROWS, LANES), jnp.bfloat16),
        in_specs=[SMEM, SMEM] + [VMEM] * 11,
        out_specs=VMEM,
        scratch_shapes=[pltpu.VMEM((groups * BOX, GROUP * BOX), jnp.bfloat16)],
        compiler_params=pltpu.CompilerParams(vmem_limit_bytes=48 << 20),
        name="crop",
    )(info, mic_defocus, labels, micrographs, jnp.asarray(left_t), jnp.asarray(right_t),
      *[jnp.asarray(t) for t in phase_tables()], ctf, jnp.asarray(lane_id[:1]), jnp.asarray(row_id))

    bank_rows, area2 = template_bank.shape
    pad_rows = -(-bank_rows // ROWS) * ROWS
    shard = template_bank.reshape(bank_rows, 2, K // 8, 8, K).transpose(0, 1, 3, 2, 4).reshape(bank_rows, area2)
    shard = jnp.pad(shard, ((0, pad_rows - bank_rows), (0, 0)))

    arrived = lax.all_to_all(outgoing, "dom", split_axis=0, concat_axis=0, tiled=True)
    bank = lax.all_gather(shard, "dom", axis=0, tiled=True)

    stride = slot_cap + 1
    got = arrived[:, slot_cap, 0, :slot_cap].astype(jnp.int32)
    at = jnp.arange(peers, dtype=jnp.int32)[:, None] * stride + jnp.arange(slot_cap, dtype=jnp.int32)[None, :]
    wanted = jnp.arange(P_DEV, dtype=jnp.int32) + 1
    where = jnp.sum(jnp.where(got[None] == wanted[:, None, None], at[None], 0), axis=(1, 2))

    flat = rot_index.reshape(-1)
    entry = flat // bank_rows * pad_rows + flat % bank_rows
    templates = flat.shape[0]
    pick = (jnp.arange(peers * pad_rows, dtype=jnp.int32)[:, None] == entry[None, :]).astype(jnp.bfloat16)

    cos_t, sin_t = shift_phases()
    full = lambda shape: pl.BlockSpec(shape, lambda i: (0,) * len(shape), pipeline_mode=pl.Buffered(1))
    out = pl.pallas_call(
        score_kernel,
        grid=(P_DEV // CHUNK,),
        out_shape=jax.ShapeDtypeStruct((P_DEV * SHIFTS, templates), jnp.bfloat16),
        in_specs=[
            SMEM,
            full((peers * stride, ROWS, LANES)),
            full((peers * pad_rows, area2)),
            full((peers * pad_rows, templates)),
            full((8, SHIFTS, LANES)),
            full((8, SHIFTS, LANES)),
        ],
        out_specs=pl.BlockSpec((CHUNK * SHIFTS, templates), lambda i: (i, 0)),
        scratch_shapes=[pltpu.VMEM((CHUNK * SHIFTS, area2), jnp.bfloat16)],
        compiler_params=pltpu.CompilerParams(vmem_limit_bytes=48 << 20),
        name="score",
    )(where, arrived.reshape(peers * stride, ROWS, LANES), bank, pick, jnp.asarray(cos_t), jnp.asarray(sin_t))
    return out.reshape(P_DEV, SHIFTS, templates)


def solution(mesh):
    return jax.shard_map(
        body,
        mesh=mesh,
        in_specs=(
            P(("groups", "dom"), None, None),
            P(("groups", "dom")),
            P("groups"),
            P(None, ("groups", "dom")),
            P(("groups", "dom"), None),
            P("groups", None),
        ),
        out_specs=P(("groups", "dom"), None, None),
        check_vma=False,
    )
```

```python
import functools
import math

import jax
import jax.numpy as jnp
import ml_dtypes
import numpy as np
from jax import lax
from jax.experimental import pallas as pl
from jax.experimental.pallas import tpu as pltpu
from jax.sharding import PartitionSpec as P

BOX = 256
K = 32
SH = 4
P_DEV = 96
SHIFTS = SH * SH
LANES = 128
ROWS = 16
GROUP = 4
CHUNK = 16

TWO_PI = 2.0 * math.pi
CHI_SCALE = 0.05
CHI_SHIFT = 0.1

MESH = pl.DeviceIdType.MESH
SUB = np.arange(8)[:, None]
LANE = np.arange(LANES)[None, :]
TILE_U = (4 * SUB + LANE // K - K // 2).astype(np.float64)
TILE_V = (LANE % K + 0 * SUB - K // 2).astype(np.float64)


def dft_tables():
    freq = np.arange(K) - K // 2
    phase = TWO_PI * np.mod(freq[:, None] * np.arange(BOX)[None, :], BOX) / BOX
    cosine = np.cos(phase) / math.sqrt(BOX)
    sine = -np.sin(phase) / math.sqrt(BOX)
    order = np.arange(K).reshape(8, K // 8).T.reshape(-1)
    left = np.concatenate([cosine[order], sine[order]], axis=0)
    right = np.zeros((GROUP, BOX, 2 * GROUP * K))
    for j in range(GROUP):
        right[j, :, j * K : (j + 1) * K] = cosine.T
        right[j, :, GROUP * K + j * K : GROUP * K + (j + 1) * K] = sine.T
    right = right.reshape(GROUP * BOX, 2 * GROUP * K)
    return left.astype(np.float32).astype(ml_dtypes.bfloat16), right.astype(np.float32).astype(ml_dtypes.bfloat16)


def phase_tables():
    rows = TWO_PI * np.arange(ROWS)[:, None, None] * TILE_U[None] / BOX
    cols = TWO_PI * np.arange(LANES)[:, None] * TILE_V[:1] / BOX
    return [f(x).astype(np.float32) for x in (rows, cols) for f in (np.cos, np.sin)]


def shift_phases():
    moves = np.arange(SH) - SH // 2
    row_move = np.repeat(moves, SH)[None, :, None]
    col_move = np.tile(moves, SH)[None, :, None]
    phase = TWO_PI * (TILE_U[:, None, :] * row_move + TILE_V[:, None, :] * col_move) / BOX
    return np.cos(phase).astype(np.float32), np.sin(phase).astype(np.float32)


def bits(n):
    return (n - 1).bit_length()


def window_tiles(q, base, shifts, info, mic, lane_id, row_id, lhs):
    label_bits, row_bits, col_bits = shifts
    scalars = []
    last_tile = mic.shape[2] - 1
    last_block = mic.shape[1] - 1
    for j in range(GROUP):
        packed = lax.shift_right_logical(info[base + j], label_bits)
        left = packed & (2**col_bits - 1)
        top = lax.shift_right_logical(packed, col_bits) & (2**row_bits - 1)
        m = lax.shift_right_logical(packed, col_bits + row_bits)
        block, rl = lax.shift_right_logical(left, 7), left & (LANES - 1)
        tile, rt = lax.shift_right_logical(top, 4), top & (ROWS - 1)
        end_tile = jnp.minimum(tile + BOX // ROWS, last_tile)
        row_f = rt.astype(jnp.float32).astype(jnp.bfloat16)
        col_f = rl.astype(jnp.float32).astype(jnp.bfloat16)

        def column(b):
            main = mic[m, b, pl.ds(tile, BOX // ROWS)].reshape(BOX, LANES)
            tail = mic[m, b, end_tile]
            head = jnp.where(row_id >= row_f, main[:ROWS], tail)
            return jnp.concatenate([head, main[ROWS:]], axis=0)

        first = column(block)
        third = column(jnp.minimum(block + 2, last_block))
        mask = lane_id >= col_f
        lhs[pl.ds(q * BOX, BOX), pl.ds(2 * j * LANES, LANES)] = jnp.where(mask, first, third)
        lhs[pl.ds(q * BOX, BOX), pl.ds((2 * j + 1) * LANES, LANES)] = column(block + 1)
        scalars.append((m, rt, rl))
    return scalars


def group_windows(grid_part, scalars, left_t, prow_c, prow_s, pcol_c, pcol_s, ctf, mic_def):
    second = jnp.dot(left_t[...], grid_part.astype(jnp.bfloat16), preferred_element_type=jnp.float32)
    real = second[:K, :LANES] - second[K:, LANES:]
    imag = second[:K, LANES:] + second[K:, :LANES]
    block_id = lax.broadcasted_iota(jnp.int32, (8, LANES), 1) // K
    tiles = []
    for j in range(GROUP):
        parts = []
        for x in (real, imag):
            total = None
            for k in range(K // 8):
                piece = x[8 * k : 8 * k + 8]
                shift = (K * (k - j)) % LANES
                piece = pltpu.roll(piece, shift, 1) if shift else piece
                total = piece if total is None else jnp.where(block_id == k, piece, total)
            parts.append(total)
        m, rt, rl = scalars[j]
        cu, su = prow_c[rt], prow_s[rt]
        cv = jnp.broadcast_to(pcol_c[pl.ds(rl, 1), :], (8, LANES))
        sv = jnp.broadcast_to(pcol_s[pl.ds(rl, 1), :], (8, LANES))
        weight = ctf[mic_def[m]]
        a = (cu * cv - su * sv) * weight
        b = (su * cv + cu * sv) * weight
        tiles.append(
            jnp.concatenate(
                [parts[0] * a - parts[1] * b, parts[0] * b + parts[1] * a], axis=0
            ).astype(jnp.bfloat16)
        )
    return tiles


def crop_kernel(peers, slot_cap, shifts, info, mic_def, defocus, shard, mic_h, left_h, right_h, prow_ch, prow_sh,
                pcol_ch, pcol_sh, arrived, bank, mic, left_t, right_t, prow_c, prow_s, pcol_c, pcol_s, ctf, lhs,
                padded, outgoing, load_sem, send_sem, recv_sem, local_sem, bank_send, bank_recv):
    groups = slot_cap // GROUP
    depth = peers // 4
    me = lax.axis_index("dom")
    my_z, my_y, my_c = me // 4, (me // 2) % 2, me % 2

    loads = [
        pltpu.make_async_copy(src, dst, load_sem.at[i])
        for i, (src, dst) in enumerate(
            [(left_h, left_t), (right_h, right_t), (prow_ch, prow_c), (prow_sh, prow_s),
             (pcol_ch, pcol_c), (pcol_sh, pcol_s)]
            + [
                (mic_h.at[m, :, :, pl.ds(b * LANES, LANES)], mic.at[m, b])
                for m in range(mic.shape[0])
                for b in range(mic.shape[1])
            ]
        )
    ]
    for load in loads:
        load.start()

    barrier = pltpu.get_barrier_semaphore()

    def greet(k, carry):
        pl.semaphore_signal(barrier, inc=1, device_id={"dom": (me + k) % peers}, device_id_type=MESH)
        return carry

    padded[...] = jnp.zeros_like(padded)
    padded[: shard.shape[0]] = shard[...]
    lax.fori_loop(1, peers, greet, 0)

    sub = lax.broadcasted_iota(jnp.int32, (8, LANES), 0)
    lane = lax.broadcasted_iota(jnp.int32, (8, LANES), 1)
    tile_u = (4 * sub + lane // K - K // 2).astype(jnp.float32)
    tile_v = (lane % K - K // 2).astype(jnp.float32)
    radius = tile_u * tile_u + tile_v * tile_v
    for d in range(defocus.shape[0]):
        ctf[d] = -jnp.sin(CHI_SCALE * defocus[d] * radius + CHI_SHIFT)
    lane_id = lax.broadcasted_iota(jnp.int32, (BOX, LANES), 1).astype(jnp.float32).astype(jnp.bfloat16)
    row_id = lax.broadcasted_iota(jnp.int32, (ROWS, LANES), 0).astype(jnp.float32).astype(jnp.bfloat16)
    label_lane = lax.broadcasted_iota(jnp.int32, (ROWS, LANES), 1)
    pl.semaphore_wait(barrier, peers - 1)

    def to_z(d):
        there = (my_z + d) % depth
        return pltpu.make_async_remote_copy(
            src_ref=padded, dst_ref=bank.at[me], send_sem=bank_send.at[d], recv_sem=bank_recv.at[d],
            device_id={"dom": there * 4 + me % 4}, device_id_type=MESH)

    def to_y(i):
        row = i * 4 + me % 4
        return pltpu.make_async_remote_copy(
            src_ref=bank.at[row], dst_ref=bank.at[row], send_sem=bank_send.at[depth + i],
            recv_sem=bank_recv.at[depth + i],
            device_id={"dom": my_z * 4 + (1 - my_y) * 2 + my_c}, device_id_type=MESH)

    def to_c(i):
        row = i * 2 + my_c
        return pltpu.make_async_remote_copy(
            src_ref=bank.at[row], dst_ref=bank.at[row], send_sem=bank_send.at[2 * depth + i],
            recv_sem=bank_recv.at[2 * depth + i],
            device_id={"dom": my_z * 4 + my_y * 2 + 1 - my_c}, device_id_type=MESH)

    def each(count, act, first=0):
        def step(i, carry):
            act(i)
            return carry

        lax.fori_loop(first, count, step, 0)

    own = pltpu.make_async_copy(padded, bank.at[me], local_sem.at[0])
    own.start()
    each(depth, lambda d: to_z(d).start(), 1)
    for load in loads:
        load.wait()

    def peer_of(k):
        step = k // 4
        dz = jnp.where(step < depth // 2, depth // 2 + step, depth - 1 - step)
        return ((my_z + dz) % depth) * 4 + (me + 1 + k) % 4

    def block_copy(k):
        return pltpu.make_async_remote_copy(
            src_ref=outgoing.at[k], dst_ref=arrived.at[me], send_sem=send_sem.at[k], recv_sem=recv_sem.at[k],
            device_id={"dom": peer_of(k)}, device_id_type=MESH)

    def per_peer(k, carry):
        base = peer_of(k) * slot_cap
        scalars = [
            window_tiles(q, base + q * GROUP, shifts, info, mic, lane_id, row_id, lhs) for q in range(groups)
        ]

        @pl.when(k > 0)
        def _():
            block_copy(k - 1).start()

        @pl.when(k == peers // 3)
        def _():
            own.wait()
            each(depth, lambda d: to_z(d).wait(), 1)
            each(depth, lambda i: to_y(i).start())

        @pl.when(k == (2 * peers) // 3)
        def _():
            each(depth, lambda i: to_y(i).wait())
            each(2 * depth, lambda i: to_c(i).start())

        first = jnp.dot(lhs[...], right_t[...], preferred_element_type=jnp.float32)
        for q in range(groups):
            tiles = group_windows(first[q * BOX : (q + 1) * BOX], scalars[q], left_t, prow_c, prow_s,
                                  pcol_c, pcol_s, ctf, mic_def)
            for j in range(GROUP):
                outgoing[k, q * GROUP + j] = tiles[j]
        labels = jnp.zeros((ROWS, LANES), jnp.int32)
        for i in range(slot_cap):
            labels = jnp.where(label_lane == i, info[base + i] & (2 ** shifts[0] - 1), labels)
        outgoing[k, slot_cap] = labels.astype(jnp.float32).astype(jnp.bfloat16)
        return carry

    lax.fori_loop(0, peers, per_peer, 0)
    mine = pltpu.make_async_copy(outgoing.at[peers - 1], arrived.at[me], local_sem.at[1])
    mine.start()
    each(2 * depth, lambda i: to_c(i).wait())
    each(peers - 1, lambda k: block_copy(k).wait())
    mine.wait()


def score_kernel(where, arrived, bank, pick, cos_t, sin_t, out, lhs):
    base = pl.program_id(0) * CHUNK

    def expand(n, carry):
        x = arrived[where[base + n]].astype(jnp.float32)
        rows = pl.ds(pl.multiple_of(n * SHIFTS, SHIFTS), SHIFTS)
        for k in range(8):
            re = jnp.broadcast_to(x[k : k + 1], (SHIFTS, LANES))
            im = jnp.broadcast_to(x[8 + k : 9 + k], (SHIFTS, LANES))
            c, s = cos_t[k], sin_t[k]
            lhs[rows, k * LANES : (k + 1) * LANES] = (re * c - im * s).astype(jnp.bfloat16)
            lhs[rows, (8 + k) * LANES : (9 + k) * LANES] = (re * s + im * c).astype(jnp.bfloat16)
        return carry

    lax.fori_loop(0, CHUNK, expand, 0, unroll=2)
    scores = lax.dot_general(lhs[...], bank[...], (((1,), (1,)), ((), ())),
                             preferred_element_type=jnp.float32).astype(jnp.bfloat16)
    out[...] = jnp.dot(scores, pick[...], preferred_element_type=jnp.float32).astype(jnp.bfloat16)


VMEM = pl.BlockSpec(memory_space=pltpu.VMEM)
HBM = pl.BlockSpec(memory_space=pl.ANY)
SMEM = pl.BlockSpec(memory_space=pltpu.SMEM)


def body(micrographs, mic_defocus, defocus, pick_list, template_bank, rot_index):
    peers = lax.axis_size("dom")
    slot_cap = (P_DEV + peers - 1) // peers * 2
    slot_cap = -(-slot_cap // GROUP) * GROUP
    mics, height, width = micrographs.shape
    label_bits, row_bits, col_bits = bits(P_DEV + 1), bits(height), bits(width)
    columns = pick_list.shape[1]

    target = pick_list[3]
    live = target >= 0
    target_dev = jnp.where(live, target // P_DEV, -1)
    label = jnp.where(live, jnp.mod(target, P_DEV) + 1, 0)
    ids = jnp.arange(columns, dtype=jnp.int32)
    earlier = (ids[None, :] < ids[:, None]) & (target_dev[None, :] == target_dev[:, None])
    rank = jnp.sum(earlier.astype(jnp.int32), axis=1)
    position = jnp.where(live, target_dev * slot_cap + rank, -1)
    mic_id = jnp.clip(pick_list[0], 0, mics - 1)
    top = jnp.clip(pick_list[1], 0, height - BOX)
    left = jnp.clip(pick_list[2], 0, width - BOX)
    packed = (((mic_id << row_bits) + top << col_bits) + left << label_bits) + label
    slots = jnp.arange(peers * slot_cap, dtype=jnp.int32)
    info = jnp.sum(jnp.where(position[None, :] == slots[:, None], packed[None, :], 0), axis=1)

    left_t, right_t = dft_tables()
    tables = [left_t, right_t] + phase_tables()
    groups = slot_cap // GROUP
    bank_rows, area2 = template_bank.shape
    pad_rows = -(-bank_rows // ROWS) * ROWS
    copies = len(tables) + mics * (width // LANES)
    dma = pltpu.SemaphoreType.DMA
    arrived, bank = pl.pallas_call(
        functools.partial(crop_kernel, peers, slot_cap, (label_bits, row_bits, col_bits)),
        out_shape=(
            jax.ShapeDtypeStruct((peers, slot_cap + 1, ROWS, LANES), jnp.bfloat16),
            jax.ShapeDtypeStruct((peers, pad_rows, area2), jnp.bfloat16),
        ),
        in_specs=[SMEM, SMEM, SMEM, VMEM] + [HBM] * (1 + len(tables)),
        out_specs=(HBM, HBM),
        scratch_shapes=[
            pltpu.VMEM((mics, width // LANES, height // ROWS, ROWS, LANES), jnp.bfloat16),
            *[pltpu.VMEM(t.shape, t.dtype) for t in tables],
            pltpu.VMEM((defocus.shape[0], 8, LANES), jnp.float32),
            pltpu.VMEM((groups * BOX, GROUP * BOX), jnp.bfloat16),
            pltpu.VMEM((pad_rows, area2), jnp.bfloat16),
            pltpu.VMEM((peers, slot_cap + 1, ROWS, LANES), jnp.bfloat16),
            dma((copies,)), dma((peers,)), dma((peers,)), dma((2,)), dma((peers,)), dma((peers,)),
        ],
        compiler_params=pltpu.CompilerParams(
            collective_id=0, has_side_effects=True, vmem_limit_bytes=56 << 20),
        name="crop",
    )(info, mic_defocus, defocus, template_bank,
      micrographs.reshape(mics, height // ROWS, ROWS, width), *[jnp.asarray(t) for t in tables])
    bank = bank.reshape(peers * pad_rows, area2)

    stride = slot_cap + 1
    got = arrived[:, slot_cap, 0, :slot_cap].astype(jnp.int32)
    at = jnp.arange(peers, dtype=jnp.int32)[:, None] * stride + jnp.arange(slot_cap, dtype=jnp.int32)[None, :]
    wanted = jnp.arange(P_DEV, dtype=jnp.int32) + 1
    where = jnp.sum(jnp.where(got[None] == wanted[:, None, None], at[None], 0), axis=(1, 2))

    flat = rot_index.reshape(-1)
    entry = flat // bank_rows * pad_rows + flat % bank_rows
    templates = flat.shape[0]
    pick = (jnp.arange(peers * pad_rows, dtype=jnp.int32)[:, None] == entry[None, :]).astype(jnp.bfloat16)

    cos_t, sin_t = shift_phases()
    full = lambda shape: pl.BlockSpec(shape, lambda i: (0,) * len(shape), pipeline_mode=pl.Buffered(1))
    out = pl.pallas_call(
        score_kernel,
        grid=(P_DEV // CHUNK,),
        out_shape=jax.ShapeDtypeStruct((P_DEV * SHIFTS, templates), jnp.bfloat16),
        in_specs=[
            SMEM,
            full((peers * stride, ROWS, LANES)),
            full((peers * pad_rows, area2)),
            full((peers * pad_rows, templates)),
            full((8, SHIFTS, LANES)),
            full((8, SHIFTS, LANES)),
        ],
        out_specs=pl.BlockSpec((CHUNK * SHIFTS, templates), lambda i: (i, 0)),
        scratch_shapes=[pltpu.VMEM((CHUNK * SHIFTS, area2), jnp.bfloat16)],
        compiler_params=pltpu.CompilerParams(vmem_limit_bytes=48 << 20),
        name="score",
    )(where, arrived.reshape(peers * stride, ROWS, LANES), bank, pick, jnp.asarray(cos_t), jnp.asarray(sin_t))
    return out.reshape(P_DEV, SHIFTS, templates)


def solution(mesh):
    return jax.shard_map(
        body,
        mesh=mesh,
        in_specs=(
            P(("groups", "dom"), None, None),
            P(("groups", "dom")),
            P("groups"),
            P(None, ("groups", "dom")),
            P(("groups", "dom"), None),
            P("groups", None),
        ),
        out_specs=P(("groups", "dom"), None, None),
        check_vma=False,
    )
```

```python
import functools
import math

import jax
import jax.numpy as jnp
import ml_dtypes
import numpy as np
from jax import lax
from jax.experimental import pallas as pl
from jax.experimental.pallas import tpu as pltpu
from jax.sharding import PartitionSpec as P

BOX = 256
K = 32
SH = 4
P_DEV = 96
SHIFTS = SH * SH
LANES = 128
ROWS = 16
GROUP = 4
CHUNK = 16
HALVES = 2

TWO_PI = 2.0 * math.pi
CHI_SCALE = 0.05
CHI_SHIFT = 0.1

MESH = pl.DeviceIdType.MESH
SUB = np.arange(8)[:, None]
LANE = np.arange(LANES)[None, :]
TILE_U = (4 * SUB + LANE // K - K // 2).astype(np.float64)
TILE_V = (LANE % K + 0 * SUB - K // 2).astype(np.float64)


def dft_tables():
    freq = np.arange(K) - K // 2
    phase = TWO_PI * np.mod(freq[:, None] * np.arange(BOX)[None, :], BOX) / BOX
    cosine = np.cos(phase) / math.sqrt(BOX)
    sine = -np.sin(phase) / math.sqrt(BOX)
    order = np.arange(K).reshape(8, K // 8).T.reshape(-1)
    left = np.concatenate([cosine[order], sine[order]], axis=0)
    right = np.zeros((GROUP, BOX, 2 * GROUP * K))
    for j in range(GROUP):
        right[j, :, j * K : (j + 1) * K] = cosine.T
        right[j, :, GROUP * K + j * K : GROUP * K + (j + 1) * K] = sine.T
    right = right.reshape(GROUP * BOX, 2 * GROUP * K)
    return left.astype(np.float32).astype(ml_dtypes.bfloat16), right.astype(np.float32).astype(ml_dtypes.bfloat16)


def phase_tables():
    rows = TWO_PI * np.arange(ROWS)[:, None, None] * TILE_U[None] / BOX
    cols = TWO_PI * np.arange(LANES)[:, None] * TILE_V[:1] / BOX
    return [f(x).astype(np.float32) for x in (rows, cols) for f in (np.cos, np.sin)]


def shift_phases():
    moves = np.arange(SH) - SH // 2
    row_move = np.repeat(moves, SH)[None, :, None]
    col_move = np.tile(moves, SH)[None, :, None]
    phase = TWO_PI * (TILE_U[:, None, :] * row_move + TILE_V[:, None, :] * col_move) / BOX
    return np.cos(phase).astype(np.float32), np.sin(phase).astype(np.float32)


def bits(n):
    return (n - 1).bit_length()


def window_tiles(q, base, shifts, info, mic, lane_id, row_id, lhs):
    label_bits, row_bits, col_bits = shifts
    scalars = []
    last_tile = mic.shape[2] - 1
    last_block = mic.shape[1] - 1
    for j in range(GROUP):
        packed = lax.shift_right_logical(info[base + j], label_bits)
        left = packed & (2**col_bits - 1)
        top = lax.shift_right_logical(packed, col_bits) & (2**row_bits - 1)
        m = lax.shift_right_logical(packed, col_bits + row_bits)
        block, rl = lax.shift_right_logical(left, 7), left & (LANES - 1)
        tile, rt = lax.shift_right_logical(top, 4), top & (ROWS - 1)
        end_tile = jnp.minimum(tile + BOX // ROWS, last_tile)
        row_f = rt.astype(jnp.float32).astype(jnp.bfloat16)
        col_f = rl.astype(jnp.float32).astype(jnp.bfloat16)

        def column(b):
            main = mic[m, b, pl.ds(tile, BOX // ROWS)].reshape(BOX, LANES)
            tail = mic[m, b, end_tile]
            head = jnp.where(row_id >= row_f, main[:ROWS], tail)
            return jnp.concatenate([head, main[ROWS:]], axis=0)

        first = column(block)
        third = column(jnp.minimum(block + 2, last_block))
        mask = lane_id >= col_f
        lhs[pl.ds(q * BOX, BOX), pl.ds(2 * j * LANES, LANES)] = jnp.where(mask, first, third)
        lhs[pl.ds(q * BOX, BOX), pl.ds((2 * j + 1) * LANES, LANES)] = column(block + 1)
        scalars.append((m, rt, rl))
    return scalars


def group_windows(grid_part, scalars, left_t, prow_c, prow_s, pcol_c, pcol_s, ctf, mic_def):
    second = jnp.dot(left_t[...], grid_part.astype(jnp.bfloat16), preferred_element_type=jnp.float32)
    real = second[:K, :LANES] - second[K:, LANES:]
    imag = second[:K, LANES:] + second[K:, :LANES]
    block_id = lax.broadcasted_iota(jnp.int32, (8, LANES), 1) // K
    tiles = []
    for j in range(GROUP):
        parts = []
        for x in (real, imag):
            total = None
            for k in range(K // 8):
                piece = x[8 * k : 8 * k + 8]
                shift = (K * (k - j)) % LANES
                piece = pltpu.roll(piece, shift, 1) if shift else piece
                total = piece if total is None else jnp.where(block_id == k, piece, total)
            parts.append(total)
        m, rt, rl = scalars[j]
        cu, su = prow_c[rt], prow_s[rt]
        cv = jnp.broadcast_to(pcol_c[pl.ds(rl, 1), :], (8, LANES))
        sv = jnp.broadcast_to(pcol_s[pl.ds(rl, 1), :], (8, LANES))
        weight = ctf[mic_def[m]]
        a = (cu * cv - su * sv) * weight
        b = (su * cv + cu * sv) * weight
        tiles.append(
            jnp.concatenate(
                [parts[0] * a - parts[1] * b, parts[0] * b + parts[1] * a], axis=0
            ).astype(jnp.bfloat16)
        )
    return tiles


def crop_kernel(peers, slot_cap, shifts, info, mic_def, defocus, shard, mic_h, left_h, right_h, prow_ch, prow_sh,
                pcol_ch, pcol_sh, arrived, bank, mic, left_t, right_t, prow_c, prow_s, pcol_c, pcol_s, ctf, lhs,
                padded, outgoing, load_sem, send_sem, recv_sem, local_sem, bank_send, bank_recv):
    groups = slot_cap // GROUP
    depth = peers // 4
    me = lax.axis_index("dom")
    my_z, my_y, my_c = me // 4, (me // 2) % 2, me % 2

    loads = [
        pltpu.make_async_copy(src, dst, load_sem.at[i])
        for i, (src, dst) in enumerate(
            [(left_h, left_t), (right_h, right_t), (prow_ch, prow_c), (prow_sh, prow_s),
             (pcol_ch, pcol_c), (pcol_sh, pcol_s)]
            + [
                (mic_h.at[m, :, :, pl.ds(b * LANES, LANES)], mic.at[m, b])
                for m in range(mic.shape[0])
                for b in range(mic.shape[1])
            ]
        )
    ]
    for load in loads:
        load.start()

    barrier = pltpu.get_barrier_semaphore()

    def greet(k, carry):
        pl.semaphore_signal(barrier, inc=1, device_id={"dom": (me + k) % peers}, device_id_type=MESH)
        return carry

    padded[...] = jnp.zeros_like(padded)
    padded[: shard.shape[0]] = shard[...]
    lax.fori_loop(1, peers, greet, 0)

    sub = lax.broadcasted_iota(jnp.int32, (8, LANES), 0)
    lane = lax.broadcasted_iota(jnp.int32, (8, LANES), 1)
    tile_u = (4 * sub + lane // K - K // 2).astype(jnp.float32)
    tile_v = (lane % K - K // 2).astype(jnp.float32)
    radius = tile_u * tile_u + tile_v * tile_v
    for d in range(defocus.shape[0]):
        ctf[d] = -jnp.sin(CHI_SCALE * defocus[d] * radius + CHI_SHIFT)
    lane_id = lax.broadcasted_iota(jnp.int32, (BOX, LANES), 1).astype(jnp.float32).astype(jnp.bfloat16)
    row_id = lax.broadcasted_iota(jnp.int32, (ROWS, LANES), 0).astype(jnp.float32).astype(jnp.bfloat16)
    label_lane = lax.broadcasted_iota(jnp.int32, (ROWS, LANES), 1)
    pl.semaphore_wait(barrier, peers - 1)

    def to_z(d):
        there = (my_z + d) % depth
        return pltpu.make_async_remote_copy(
            src_ref=padded, dst_ref=bank.at[me], send_sem=bank_send.at[d], recv_sem=bank_recv.at[d],
            device_id={"dom": there * 4 + me % 4}, device_id_type=MESH)

    def to_y(i):
        row = i * 4 + me % 4
        return pltpu.make_async_remote_copy(
            src_ref=bank.at[row], dst_ref=bank.at[row], send_sem=bank_send.at[depth + i],
            recv_sem=bank_recv.at[depth + i],
            device_id={"dom": my_z * 4 + (1 - my_y) * 2 + my_c}, device_id_type=MESH)

    def to_c(i):
        row = i * 2 + my_c
        return pltpu.make_async_remote_copy(
            src_ref=bank.at[row], dst_ref=bank.at[row], send_sem=bank_send.at[2 * depth + i],
            recv_sem=bank_recv.at[2 * depth + i],
            device_id={"dom": my_z * 4 + my_y * 2 + 1 - my_c}, device_id_type=MESH)

    def each(count, act, first=0):
        def step(i, carry):
            act(i)
            return carry

        lax.fori_loop(first, count, step, 0)

    own = pltpu.make_async_copy(padded, bank.at[me], local_sem.at[0])
    own.start()
    each(depth, lambda d: to_z(d).start(), 1)
    for load in loads:
        load.wait()

    def peer_of(k):
        step = k // 4
        dz = jnp.where(step < depth // 2, depth // 2 + step, depth - 1 - step)
        return ((my_z + dz) % depth) * 4 + (me + 1 + k) % 4

    def block_copy(k):
        return pltpu.make_async_remote_copy(
            src_ref=outgoing.at[k], dst_ref=arrived.at[me], send_sem=send_sem.at[k], recv_sem=recv_sem.at[k],
            device_id={"dom": peer_of(k)}, device_id_type=MESH)

    def per_peer(k, carry):
        base = peer_of(k) * slot_cap
        scalars = [
            window_tiles(q, base + q * GROUP, shifts, info, mic, lane_id, row_id, lhs) for q in range(groups)
        ]

        @pl.when(k > 0)
        def _():
            block_copy(k - 1).start()

        @pl.when(k == peers // 3)
        def _():
            own.wait()
            each(depth, lambda d: to_z(d).wait(), 1)
            each(depth, lambda i: to_y(i).start())

        @pl.when(k == peers - 2)
        def _():
            each(depth, lambda i: to_y(i).wait())
            each(2 * depth, lambda i: to_c(i).start())

        first = jnp.dot(lhs[...], right_t[...], preferred_element_type=jnp.float32)
        for q in range(groups):
            tiles = group_windows(first[q * BOX : (q + 1) * BOX], scalars[q], left_t, prow_c, prow_s,
                                  pcol_c, pcol_s, ctf, mic_def)
            for j in range(GROUP):
                outgoing[k, q * GROUP + j] = tiles[j]
        labels = jnp.zeros((ROWS, LANES), jnp.int32)
        for i in range(slot_cap):
            labels = jnp.where(label_lane == i, info[base + i] & (2 ** shifts[0] - 1), labels)
        outgoing[k, slot_cap] = labels.astype(jnp.float32).astype(jnp.bfloat16)
        return carry

    lax.fori_loop(0, peers, per_peer, 0)
    mine = pltpu.make_async_copy(outgoing.at[peers - 1], arrived.at[me], local_sem.at[1])
    mine.start()
    each(2 * depth, lambda i: to_c(i).wait())
    each(peers - 1, lambda k: block_copy(k).wait())
    mine.wait()


def score_kernel(where, arrived, bank, pick, cos_t, sin_t, out, *halves):
    base = pl.program_id(0) * CHUNK * len(halves)

    def expand(half, lhs):
        for n in range(CHUNK):
            x = arrived[where[base + half * CHUNK + n]].astype(jnp.float32)
            rows = slice(n * SHIFTS, (n + 1) * SHIFTS)
            for k in range(8):
                re = jnp.broadcast_to(x[k : k + 1], (SHIFTS, LANES))
                im = jnp.broadcast_to(x[8 + k : 9 + k], (SHIFTS, LANES))
                c, s = cos_t[k], sin_t[k]
                lhs[rows, k * LANES : (k + 1) * LANES] = (re * c - im * s).astype(jnp.bfloat16)
                lhs[rows, (8 + k) * LANES : (9 + k) * LANES] = (re * s + im * c).astype(jnp.bfloat16)

    def score(lhs):
        return lax.dot_general(lhs[...], bank[...], (((1,), (1,)), ((), ())),
                               preferred_element_type=jnp.float32).astype(jnp.bfloat16)

    def emit(half, scores):
        rows = CHUNK * SHIFTS
        picked = jnp.dot(scores, pick[...], preferred_element_type=jnp.float32)
        out[half * rows : (half + 1) * rows] = picked.astype(jnp.bfloat16)

    waiting = None
    for half, lhs in enumerate(halves):
        expand(half, lhs)
        scores = score(lhs)
        if waiting is not None:
            emit(half - 1, waiting)
        waiting = scores
    emit(len(halves) - 1, waiting)


VMEM = pl.BlockSpec(memory_space=pltpu.VMEM)
HBM = pl.BlockSpec(memory_space=pltpu.HBM)
ANY = pl.BlockSpec(memory_space=pl.ANY)
SMEM = pl.BlockSpec(memory_space=pltpu.SMEM)


def body(micrographs, mic_defocus, defocus, pick_list, template_bank, rot_index):
    peers = lax.axis_size("dom")
    slot_cap = (P_DEV + peers - 1) // peers * 2
    slot_cap = -(-slot_cap // GROUP) * GROUP
    mics, height, width = micrographs.shape
    label_bits, row_bits, col_bits = bits(P_DEV + 1), bits(height), bits(width)
    columns = pick_list.shape[1]

    target = pick_list[3]
    live = target >= 0
    target_dev = jnp.where(live, target // P_DEV, -1)
    label = jnp.where(live, jnp.mod(target, P_DEV) + 1, 0)
    ids = jnp.arange(columns, dtype=jnp.int32)
    earlier = (ids[None, :] < ids[:, None]) & (target_dev[None, :] == target_dev[:, None])
    rank = jnp.sum(earlier.astype(jnp.int32), axis=1)
    position = jnp.where(live, target_dev * slot_cap + rank, -1)
    mic_id = jnp.clip(pick_list[0], 0, mics - 1)
    top = jnp.clip(pick_list[1], 0, height - BOX)
    left = jnp.clip(pick_list[2], 0, width - BOX)
    packed = (((mic_id << row_bits) + top << col_bits) + left << label_bits) + label
    slots = jnp.arange(peers * slot_cap, dtype=jnp.int32)
    info = jnp.sum(jnp.where(position[None, :] == slots[:, None], packed[None, :], 0), axis=1)

    left_t, right_t = dft_tables()
    tables = [left_t, right_t] + phase_tables()
    groups = slot_cap // GROUP
    bank_rows, area2 = template_bank.shape
    pad_rows = -(-bank_rows // ROWS) * ROWS
    copies = len(tables) + mics * (width // LANES)
    dma = pltpu.SemaphoreType.DMA
    arrived, bank = pl.pallas_call(
        functools.partial(crop_kernel, peers, slot_cap, (label_bits, row_bits, col_bits)),
        out_shape=(
            jax.ShapeDtypeStruct((peers, slot_cap + 1, ROWS, LANES), jnp.bfloat16),
            jax.ShapeDtypeStruct((peers, pad_rows, area2), jnp.bfloat16),
        ),
        in_specs=[SMEM, SMEM, SMEM, VMEM] + [HBM] * (1 + len(tables)),
        out_specs=(ANY, ANY),
        scratch_shapes=[
            pltpu.VMEM((mics, width // LANES, height // ROWS, ROWS, LANES), jnp.bfloat16),
            *[pltpu.VMEM(t.shape, t.dtype) for t in tables],
            pltpu.VMEM((defocus.shape[0], 8, LANES), jnp.float32),
            pltpu.VMEM((groups * BOX, GROUP * BOX), jnp.bfloat16),
            pltpu.VMEM((pad_rows, area2), jnp.bfloat16),
            pltpu.VMEM((peers, slot_cap + 1, ROWS, LANES), jnp.bfloat16),
            dma((copies,)), dma((peers,)), dma((peers,)), dma((2,)), dma((peers,)), dma((peers,)),
        ],
        compiler_params=pltpu.CompilerParams(
            collective_id=0, has_side_effects=True, vmem_limit_bytes=56 << 20),
        name="crop",
    )(info, mic_defocus, defocus, template_bank,
      micrographs.reshape(mics, height // ROWS, ROWS, width), *[jnp.asarray(t) for t in tables])
    bank = bank.reshape(peers * pad_rows, area2)

    stride = slot_cap + 1
    got = arrived[:, slot_cap, 0, :slot_cap].astype(jnp.int32)
    at = jnp.arange(peers, dtype=jnp.int32)[:, None] * stride + jnp.arange(slot_cap, dtype=jnp.int32)[None, :]
    wanted = jnp.arange(P_DEV, dtype=jnp.int32) + 1
    where = jnp.sum(jnp.where(got[None] == wanted[:, None, None], at[None], 0), axis=(1, 2))

    flat = rot_index.reshape(-1)
    entry = flat + lax.div(flat, jnp.int32(bank_rows)) * (pad_rows - bank_rows)
    templates = flat.shape[0]
    pick = (jnp.arange(peers * pad_rows, dtype=jnp.int32)[:, None] == entry[None, :]).astype(jnp.bfloat16)

    cos_t, sin_t = shift_phases()
    full = lambda shape: pl.BlockSpec(shape, lambda i: (0,) * len(shape), pipeline_mode=pl.Buffered(1))
    out = pl.pallas_call(
        score_kernel,
        grid=(P_DEV // (HALVES * CHUNK),),
        out_shape=jax.ShapeDtypeStruct((P_DEV * SHIFTS, templates), jnp.bfloat16),
        in_specs=[
            SMEM,
            full((peers * stride, ROWS, LANES)),
            full((peers * pad_rows, area2)),
            full((peers * pad_rows, templates)),
            full((8, SHIFTS, LANES)),
            full((8, SHIFTS, LANES)),
        ],
        out_specs=pl.BlockSpec((HALVES * CHUNK * SHIFTS, templates), lambda i: (i, 0)),
        scratch_shapes=[pltpu.VMEM((CHUNK * SHIFTS, area2), jnp.bfloat16)] * HALVES,
        compiler_params=pltpu.CompilerParams(vmem_limit_bytes=56 << 20),
        name="score",
    )(where, arrived.reshape(peers * stride, ROWS, LANES), bank, pick, jnp.asarray(cos_t), jnp.asarray(sin_t))
    return out.reshape(P_DEV, SHIFTS, templates)


def solution(mesh):
    return jax.shard_map(
        body,
        mesh=mesh,
        in_specs=(
            P(("groups", "dom"), None, None),
            P(("groups", "dom")),
            P("groups"),
            P(None, ("groups", "dom")),
            P(("groups", "dom"), None),
            P("groups", None),
        ),
        out_specs=P(("groups", "dom"), None, None),
        check_vma=False,
    )
```
